32 devices in a mesh: ctx: 4 (over y, core), fsdp: 8 (over z, x).
Axes of the slice: x: 2, y: 2, z: 4, core: 2. Of those that a mesh axis runs over, the one named last changes fastest.
Arguments:
- block_input: bfloat16 [8, 1024, 768], P('fsdp', 'ctx'), may hold values from -6 to 6
- cotangent: bfloat16 [8, 1024, 768], P('fsdp', 'ctx'), may hold values from -6 to 6
- attend_gain: bfloat16 [2, 768], P(None, 'fsdp'), may hold values from 0.5 to 1.5
- attend_shift: bfloat16 [2, 768], P(None, 'fsdp'), may hold values from -3 to 3
- joint_weight: bfloat16 [2, 768, 2304], P(None, 'fsdp'), may hold values from -0.21875 to 0.21875
- query_bias: bfloat16 [2, 768], P(None, 'fsdp'), may hold values from -3 to 3
- value_bias: bfloat16 [2, 768], P(None, 'fsdp'), may hold values from -3 to 3
- mixer_weight: bfloat16 [2, 768, 768], P(None, 'fsdp'), may hold values from -0.75 to 0.75
- mixer_bias: bfloat16 [2, 768], P(None, 'fsdp'), may hold values from -3 to 3
- feed_gain: bfloat16 [2, 768], P(None, 'fsdp'), may hold values from 0.5 to 1.5
- feed_shift: bfloat16 [2, 768], P(None, 'fsdp'), may hold values from -3 to 3
- expand_weight: bfloat16 [2, 768, 3072], P(None, 'fsdp'), may hold values from -0.21875 to 0.21875
- expand_bias: bfloat16 [2, 3072], P(None, 'fsdp'), may hold values from -3 to 3
- reduce_weight: bfloat16 [2, 3072, 768], P(None, 'fsdp'), may hold values from -0.109375 to 0.109375
- reduce_bias: bfloat16 [2, 768], P(None, 'fsdp'), may hold values from -3 to 3
Outputs:
- block_output: float32 [8, 1024, 768], P('fsdp', 'ctx')
- input_grad: float32 [8, 1024, 768], P('fsdp', 'ctx')
- attend_gain_grad: float32 [2, 768], P(None, 'fsdp')
- attend_shift_grad: float32 [2, 768], P(None, 'fsdp')
- joint_weight_grad: float32 [2, 768, 2304], P(None, 'fsdp')
- query_bias_grad: float32 [2, 768], P(None, 'fsdp')
- value_bias_grad: float32 [2, 768], P(None, 'fsdp')
- mixer_weight_grad: float32 [2, 768, 768], P(None, 'fsdp')
- mixer_bias_grad: float32 [2, 768], P(None, 'fsdp')
- feed_gain_grad: float32 [2, 768], P(None, 'fsdp')
- feed_shift_grad: float32 [2, 768], P(None, 'fsdp')
- expand_weight_grad: float32 [2, 768, 3072], P(None, 'fsdp')
- expand_bias_grad: float32 [2, 3072], P(None, 'fsdp')
- reduce_weight_grad: float32 [2, 3072, 768], P(None, 'fsdp')
- reduce_bias_grad: float32 [2, 768], P(None, 'fsdp')
The draws below stay inside these ranges and needn't reach their ends.
All inputs are finite; a program needn't handle non-finite values.
Results may differ from the reference program's by a relative error of at most 0.04.
Values may be sent and summed in bfloat16 or wider, within the bound.
A program may use at most 192 MiB of HBM per device.

```python
import math
import jax
import jax.numpy as jnp
from jax import lax

HEADS = 12
HDIM = 64
D = 768
FF = 3072
SEQ_LEN = 1024
LAYERS = 2
SEQS = 8


def block_levels(stream_key, shape, cuts, smallest, high):
    loudness = 1.0
    for dim, shards_of in cuts:
        steps = jax.random.uniform(jax.random.fold_in(jax.random.fold_in(stream_key, 6), dim), (shards_of,), jnp.float32, smallest / len(cuts), high / len(cuts))
        loudness = loudness * jnp.repeat(jnp.exp(steps), shape[dim] // shards_of).reshape((-1,) + (1,) * (len(shape) - 1 - dim))
    return loudness


def noise(rng, shape, spread, most, split=(), kind=jnp.bfloat16):
    values = jax.random.normal(rng, shape, jnp.float32) * spread
    if len(split) > 0:
        values = block_levels(rng, shape, split, -0.22, 0.18) * values
    return jnp.clip(values, min=-most, max=most).astype(kind)


def setup_inputs(seed: int = 0) -> dict:
    key_list = jax.random.split(jax.random.key(seed), 16)
    block_input = noise(key_list[0], (SEQS, SEQ_LEN, D), 1.0, 6.0, ((0, 8), (1, 4)))
    cotangent = noise(key_list[1], (SEQS, SEQ_LEN, D), 1.0, 6.0, ((0, 8), (1, 4)))
    attend_gain = jnp.clip(1.0 + 0.1 * jax.random.normal(key_list[2], (LAYERS, D), jnp.float32), 0.5, 1.5).astype(jnp.bfloat16)
    attend_shift = noise(key_list[3], (LAYERS, D), 0.5, 3.0, ((1, 8),))
    joint_weight = noise(key_list[4], (LAYERS, D, 3 * D), D ** -0.5, 0.21875, ((1, 8),))
    query_bias = noise(key_list[5], (LAYERS, D), 0.5, 3.0, ((1, 8),))
    value_bias = noise(key_list[6], (LAYERS, D), 0.5, 3.0, ((1, 8),))
    mixer_weight = noise(key_list[7], (LAYERS, D, D), HDIM ** -0.5, 0.75, ((1, 8),))
    mixer_bias = noise(key_list[8], (LAYERS, D), 0.5, 3.0, ((1, 8),))
    feed_gain = jnp.clip(1.0 + 0.1 * jax.random.normal(key_list[9], (LAYERS, D), jnp.float32), 0.5, 1.5).astype(jnp.bfloat16)
    feed_shift = noise(key_list[10], (LAYERS, D), 0.5, 3.0, ((1, 8),))
    expand_weight = noise(key_list[11], (LAYERS, D, FF), D ** -0.5, 0.21875, ((1, 8),))
    expand_bias = noise(key_list[12], (LAYERS, FF), 0.5, 3.0, ((1, 8),))
    reduce_weight = noise(key_list[13], (LAYERS, FF, D), FF ** -0.5, 0.109375, ((1, 8),))
    reduce_bias = noise(key_list[14], (LAYERS, D), 0.5, 3.0, ((1, 8),))
    return {"block_input": block_input, "cotangent": cotangent, "attend_gain": attend_gain, "attend_shift": attend_shift, "joint_weight": joint_weight, "query_bias": query_bias, "value_bias": value_bias, "mixer_weight": mixer_weight, "mixer_bias": mixer_bias, "feed_gain": feed_gain, "feed_shift": feed_shift, "expand_weight": expand_weight, "expand_bias": expand_bias, "reduce_weight": reduce_weight, "reduce_bias": reduce_bias}


EPS = 1e-05
GELU_C = math.sqrt(2.0 / math.pi)

def mix(form, left, right):
    return jnp.einsum(form, left.astype(jnp.float32), right.astype(jnp.float32))

def norm_forward(stream, gain, shift):
    centred = stream - lax.optimization_barrier(jnp.mean(stream, axis=-1, keepdims=True))
    inverse = lax.rsqrt(lax.optimization_barrier(jnp.mean(centred * centred, axis=-1, keepdims=True)) + EPS)
    scaled = centred * inverse
    return (scaled * gain.astype(jnp.float32) + shift.astype(jnp.float32), scaled, inverse)

def norm_backward(upstream, scaled, inverse, gain):
    weighted = upstream * gain.astype(jnp.float32)
    inner = weighted - lax.optimization_barrier(jnp.mean(weighted, axis=-1, keepdims=True)) - scaled * lax.optimization_barrier(jnp.mean(weighted * scaled, axis=-1, keepdims=True))
    return (inverse * inner, lax.optimization_barrier(jnp.sum(upstream * scaled, axis=0)), lax.optimization_barrier(jnp.sum(upstream, axis=0)))

def gelu_parts(hidden):
    cube = hidden * hidden * hidden
    tangent = jnp.tanh(GELU_C * (hidden + 0.044715 * cube))
    value = 0.5 * hidden * (1.0 + tangent)
    slope = 0.5 * (1.0 + tangent) + 0.5 * hidden * (1.0 - tangent * tangent) * GELU_C * (1.0 + 3.0 * 0.044715 * hidden * hidden)
    return (value, slope)

def block_scores(queries, keys_all, start, block, scale):
    end = start + block
    scores = mix('sqgd,skgd->sgqk', queries[:, start:end], keys_all[:, :end]) * scale
    rows = start + jnp.arange(block)[:, None]
    columns = jnp.arange(end)[None, :]
    visible = columns <= rows
    return (jnp.where(visible, scores, -1e+30), visible)

def attend_forward(queries, keys_all, values_all):
    length = queries.shape[1]
    block = min(512, length)
    scale = 1.0 / math.sqrt(queries.shape[-1])
    outputs = []
    totals = []
    for index in range(length // block):
        start = index * block
        scores, visible = block_scores(queries, keys_all, start, block, scale)
        peak = lax.optimization_barrier(jnp.max(scores, axis=-1, keepdims=True))
        logsum = peak + jnp.log(lax.optimization_barrier(jnp.sum(jnp.exp(scores - peak), axis=-1, keepdims=True)))
        probs = jnp.exp(scores - logsum).astype(jnp.bfloat16)
        outputs.append(mix('sgqk,skgd->sqgd', probs, values_all[:, :start + block]).astype(jnp.bfloat16))
        totals.append(logsum[..., 0])
    return (jnp.concatenate(outputs, axis=1), jnp.concatenate(totals, axis=2))

def attend_backward(queries, keys_all, values_all, outputs, logsum, out_grad):
    length = queries.shape[1]
    block = min(512, length)
    scale = 1.0 / math.sqrt(queries.shape[-1])
    query_parts = []
    key_grad = jnp.zeros(keys_all.shape, jnp.float32)
    value_grad = jnp.zeros(values_all.shape, jnp.float32)
    for index in range(length // block):
        start = index * block
        end = start + block
        scores, visible = block_scores(queries, keys_all, start, block, scale)
        probs = jnp.where(visible, jnp.exp(scores - logsum[:, :, start:end, None]), 0.0)
        grad_block = out_grad[:, start:end]
        value_grad = value_grad.at[:, :end].add(mix('sgqk,sqgd->skgd', probs.astype(jnp.bfloat16), grad_block))
        prob_grad = mix('sqgd,skgd->sgqk', grad_block, values_all[:, :end])
        delta = lax.optimization_barrier(jnp.sum(grad_block.astype(jnp.float32) * outputs[:, start:end].astype(jnp.float32), axis=-1))
        delta = jnp.transpose(delta, (0, 2, 1))[..., None]
        score_grad = (probs * (prob_grad - delta)).astype(jnp.bfloat16)
        query_parts.append(mix('sgqk,skgd->sqgd', score_grad, keys_all[:, :end]) * scale)
        key_grad = key_grad.at[:, :end].add(mix('sgqk,sqgd->skgd', score_grad, queries[:, start:end]) * scale)
    query_grad = jnp.concatenate(query_parts, axis=1)
    return jnp.stack([query_grad, key_grad, value_grad], axis=2).astype(jnp.bfloat16)

def layer_forward(stream, params):
    att_gain, att_shift, joint_w, query_b, value_b, mixer_w, mixer_b, feed_g, feed_s, expand_w, expand_b, reduce_w, reduce_b = params
    normed, scaled_one, inverse_one = norm_forward(stream, att_gain, att_shift)
    first = normed.astype(jnp.bfloat16)
    bias_row = jnp.concatenate([query_b.astype(jnp.float32), jnp.zeros((D,), jnp.float32), value_b.astype(jnp.float32)])
    joint = (jnp.dot(first, joint_w, preferred_element_type=jnp.float32) + bias_row).astype(jnp.bfloat16)
    heads = joint.reshape(SEQS, SEQ_LEN, 3, HEADS, HDIM)

    def one_sequence(single):
        outs, sums = attend_forward(single[None, :, 0], single[None, :, 1], single[None, :, 2])
        return (outs[0], sums[0])
    attended_heads, logsum = lax.map(one_sequence, heads)
    attended = attended_heads.reshape(SEQS * SEQ_LEN, D)
    middle = stream + jnp.dot(attended, mixer_w, preferred_element_type=jnp.float32) + mixer_b.astype(jnp.float32)
    normed_two, scaled_two, inverse_two = norm_forward(middle, feed_g, feed_s)
    second = normed_two.astype(jnp.bfloat16)
    hidden = jnp.dot(second, expand_w, preferred_element_type=jnp.float32) + expand_b.astype(jnp.float32)
    value, slope = gelu_parts(hidden)
    active = value.astype(jnp.bfloat16)
    result = middle + jnp.dot(active, reduce_w, preferred_element_type=jnp.float32) + reduce_b.astype(jnp.float32)
    kept = (scaled_one, inverse_one, first, heads, attended_heads, logsum, attended, scaled_two, inverse_two, second, slope, active)
    return (result, kept)

def layer_backward(upstream, kept, params):
    att_gain, att_shift, joint_w, query_b, value_b, mixer_w, mixer_b, feed_g, feed_s, expand_w, expand_b, reduce_w, reduce_b = params
    scaled_one, inverse_one, first, heads, attended_heads, logsum, attended, scaled_two, inverse_two, second, slope, active = kept
    upstream_b = upstream.astype(jnp.bfloat16)
    reduce_b_grad = lax.optimization_barrier(jnp.sum(upstream, axis=0))
    reduce_w_grad = jnp.dot(active.T, upstream_b, preferred_element_type=jnp.float32)
    hidden_grad = jnp.dot(upstream_b, reduce_w.T, preferred_element_type=jnp.float32) * slope
    expand_b_grad = lax.optimization_barrier(jnp.sum(hidden_grad, axis=0))
    hidden_b = hidden_grad.astype(jnp.bfloat16)
    expand_w_grad = jnp.dot(second.T, hidden_b, preferred_element_type=jnp.float32)
    into_norm = jnp.dot(hidden_b, expand_w.T, preferred_element_type=jnp.float32)
    norm_grad, feed_g_grad, feed_s_grad = norm_backward(into_norm, scaled_two, inverse_two, feed_g)
    middle_grad = upstream + norm_grad
    middle_b = middle_grad.astype(jnp.bfloat16)
    mixer_b_grad = lax.optimization_barrier(jnp.sum(middle_grad, axis=0))
    mixer_w_grad = jnp.dot(attended.T, middle_b, preferred_element_type=jnp.float32)
    attended_grad = jnp.dot(middle_b, mixer_w.T, preferred_element_type=jnp.float32).astype(jnp.bfloat16)
    grad_heads = attended_grad.reshape(SEQS, SEQ_LEN, HEADS, HDIM)

    def one_sequence(items):
        single, outs, sums, grads = items
        joint_g = attend_backward(single[None, :, 0], single[None, :, 1], single[None, :, 2], outs[None], sums[None], grads[None])
        return joint_g[0]
    joint_heads_grad = lax.map(one_sequence, (heads, attended_heads, logsum, grad_heads))
    joint_grad = joint_heads_grad.reshape(SEQS * SEQ_LEN, 3 * D)
    joint_w_grad = jnp.dot(first.T, joint_grad, preferred_element_type=jnp.float32)
    joint_sums = lax.optimization_barrier(jnp.sum(joint_grad.astype(jnp.float32), axis=0))
    query_b_grad = joint_sums[:D]
    value_b_grad = joint_sums[2 * D:]
    into_first = jnp.dot(joint_grad, joint_w.T, preferred_element_type=jnp.float32)
    first_grad, att_gain_grad, att_shift_grad = norm_backward(into_first, scaled_one, inverse_one, att_gain)
    grads = (att_gain_grad, att_shift_grad, joint_w_grad, query_b_grad, value_b_grad, mixer_w_grad, mixer_b_grad, feed_g_grad, feed_s_grad, expand_w_grad, expand_b_grad, reduce_w_grad, reduce_b_grad)
    return (middle_grad + first_grad, grads)

def reference(block_input, cotangent, attend_gain, attend_shift, joint_weight, query_bias, value_bias, mixer_weight, mixer_bias, feed_gain, feed_shift, expand_weight, expand_bias, reduce_weight, reduce_bias):
    stacked = (attend_gain, attend_shift, joint_weight, query_bias, value_bias, mixer_weight, mixer_bias, feed_gain, feed_shift, expand_weight, expand_bias, reduce_weight, reduce_bias)
    stream = block_input.astype(jnp.float32).reshape(SEQS * SEQ_LEN, D)
    saved = []
    for layer in range(LAYERS):
        params = tuple((item[layer] for item in stacked))
        stream, kept = layer_forward(stream, params)
        saved.append(kept)
    upstream = cotangent.astype(jnp.float32).reshape(SEQS * SEQ_LEN, D)
    layer_grads = [None] * LAYERS
    for layer in reversed(range(LAYERS)):
        params = tuple((item[layer] for item in stacked))
        upstream, grads = layer_backward(upstream, saved[layer], params)
        layer_grads[layer] = grads
    gathered = tuple((jnp.stack([layer_grads[layer][index] for layer in range(LAYERS)]) for index in range(13)))
    output = stream.reshape(SEQS, SEQ_LEN, D)
    in_grad = upstream.reshape(SEQS, SEQ_LEN, D)
    return (output, in_grad, gathered[0], gathered[1], gathered[2], gathered[3], gathered[4], gathered[5], gathered[6], gathered[7], gathered[8], gathered[9], gathered[10], gathered[11], gathered[12])
```

```python
import functools
import math

import jax
import jax.numpy as jnp
from jax import lax
from jax.experimental import pallas as pl
from jax.experimental.pallas import tpu as pltpu
from jax.sharding import PartitionSpec as P

HDIM = 64
LAYERS = 2
EPS = 1e-05
GELU_C = math.sqrt(2.0 / math.pi)
BF = jnp.bfloat16
F32 = jnp.float32
SCALE = 1.0 / math.sqrt(HDIM)


def dot(a, b, da, db):
    return lax.dot_general(a, b, (((da,), (db,)), ((), ())), preferred_element_type=F32)


def norm_forward(stream, gain, shift):
    centred = stream - jnp.mean(stream, axis=-1, keepdims=True)
    inverse = lax.rsqrt(jnp.mean(centred * centred, axis=-1, keepdims=True) + EPS)
    scaled = centred * inverse
    return (scaled * gain + shift, scaled, inverse)


def norm_backward(upstream, scaled, inverse, gain):
    weighted = upstream * gain
    inner = (
        weighted
        - jnp.mean(weighted, axis=-1, keepdims=True)
        - scaled * jnp.mean(weighted * scaled, axis=-1, keepdims=True)
    )
    return (inverse * inner, jnp.sum(upstream * scaled, axis=0), jnp.sum(upstream, axis=0))


def gelu_parts(hidden):
    cube = hidden * hidden * hidden
    tangent = jnp.tanh(GELU_C * (hidden + 0.044715 * cube))
    value = 0.5 * hidden * (1.0 + tangent)
    slope = 0.5 * (1.0 + tangent) + 0.5 * hidden * (1.0 - tangent * tangent) * GELU_C * (
        1.0 + 3.0 * 0.044715 * hidden * hidden
    )
    return (value, slope)


def masked_scores(q, k, start):
    scores = dot(q, k, 1, 1) * SCALE
    rows = start + lax.broadcasted_iota(jnp.int32, scores.shape, 0)
    columns = lax.broadcasted_iota(jnp.int32, scores.shape, 1)
    return jnp.where(columns <= rows, scores, -1e30)


def forward_kernel(block, q_ref, k_ref, v_ref, o_ref):
    for start in range(0, q_ref.shape[0], block):
        end = start + block
        scores = masked_scores(q_ref[start:end, :], k_ref[:end, :], start)
        peak = jnp.max(scores, axis=-1, keepdims=True)
        weights = jnp.exp(scores - peak)
        probs = (weights * (1.0 / jnp.sum(weights, axis=-1, keepdims=True))).astype(BF)
        o_ref[start:end, :] = dot(probs, v_ref[:end, :], 1, 0).astype(BF)


def backward_kernel(block, q_ref, k_ref, v_ref, o_ref, g_ref, dq_ref, dk_ref, dv_ref, ka, va):
    length = q_ref.shape[0]
    for start in reversed(range(0, length, block)):
        end = start + block
        q, k, v, g = q_ref[start:end, :], k_ref[:end, :], v_ref[:end, :], g_ref[start:end, :]
        scores = masked_scores(q, k, start)
        peak = jnp.max(scores, axis=-1, keepdims=True)
        weights = jnp.exp(scores - peak)
        probs = weights * (1.0 / jnp.sum(weights, axis=-1, keepdims=True))
        dv = dot(probs.astype(BF), g, 0, 0)
        delta = jnp.sum(g.astype(F32) * o_ref[start:end, :].astype(F32), axis=-1, keepdims=True)
        ds = (probs * (dot(g, v, 1, 1) - delta)).astype(BF)
        dq_ref[start:end, :] = (dot(ds, k, 1, 0) * SCALE).astype(BF)
        dk = dot(ds, q, 0, 0) * SCALE
        if end == length:
            ka[...] = dk
            va[...] = dv
        else:
            ka[:end, :] += dk
            va[:end, :] += dv
    dk_ref[...] = ka[...].astype(BF)
    dv_ref[...] = va[...].astype(BF)


def head_spec(length, offset):
    return pl.BlockSpec((None, None, length, HDIM), lambda s, h: (s, h + offset, 0, 0))


def attend_forward(joint):
    items, nine, length, _ = joint.shape
    group = nine // 3
    return pl.pallas_call(
        functools.partial(forward_kernel, length // 2),
        grid=(items, group),
        in_specs=[head_spec(length, part * group) for part in range(3)],
        out_specs=head_spec(length, 0),
        out_shape=jax.ShapeDtypeStruct((items, group, length, HDIM), BF),
        cost_estimate=pl.CostEstimate(
            flops=3 * items * group * length * length * HDIM,
            bytes_accessed=8 * items * group * length * HDIM,
            transcendentals=items * group * length * length,
        ),
    )(joint, joint, joint)


def attend_backward(joint, attended, grad):
    items, nine, length, _ = joint.shape
    group = nine // 3
    out = jax.ShapeDtypeStruct((items, group, length, HDIM), BF)
    return pl.pallas_call(
        functools.partial(backward_kernel, length // 2),
        grid=(items, group),
        in_specs=[head_spec(length, part * group) for part in range(3)]
        + [head_spec(length, 0)] * 2,
        out_specs=[head_spec(length, 0)] * 3,
        out_shape=[out] * 3,
        scratch_shapes=[pltpu.VMEM((length, HDIM), F32)] * 2,
        cost_estimate=pl.CostEstimate(
            flops=8 * items * group * length * length * HDIM,
            bytes_accessed=16 * items * group * length * HDIM,
            transcendentals=items * group * length * length,
        ),
    )(joint, joint, joint, attended, grad)


def swap(array, partner):
    return lax.ppermute(array, "ctx", [(i, i ^ partner) for i in range(4)])


def gather_relative(own):
    across = swap(own, 2)
    beside = swap(own, 1)
    return jnp.stack([own, beside, across, swap(across, 1)])


def reorder(blocks, me):
    return jnp.stack(
        [lax.dynamic_index_in_dim(blocks, me ^ r, 0, keepdims=False) for r in range(4)]
    )


def gather_ctx(own, me):
    return reorder(gather_relative(own), me)


def scatter_relative(blocks):
    low = blocks.astype(BF)
    got = swap(jnp.stack([low[1], low[3]]), 1).astype(F32)
    mine = blocks[0].astype(F32) + got[0]
    other = (blocks[2].astype(F32) + got[1]).astype(BF)
    return mine + swap(other, 2).astype(F32)


def body(
    block_input,
    cotangent,
    attend_gain,
    attend_shift,
    joint_weight,
    query_bias,
    value_bias,
    mixer_weight,
    mixer_bias,
    feed_gain,
    feed_shift,
    expand_weight,
    expand_bias,
    reduce_weight,
    reduce_bias,
):
    me = lax.axis_index("ctx")
    parts = 4
    shards = lax.axis_size("fsdp")
    seqs, piece, width = block_input.shape
    rows = seqs * piece
    tokens = rows * parts
    length = piece * parts
    slim = width // parts
    group = slim // HDIM
    shard = width // shards
    hidden_shard = reduce_weight.shape[1]
    unit = hidden_shard // parts
    units = unit * shards
    pad_rows = 8

    def own_joint(layer):
        joint = lax.dynamic_index_in_dim(
            joint_weight[layer].reshape(shard, 3, parts, slim), me, 2, keepdims=False
        ).reshape(shard, 3 * slim)
        mixer = lax.dynamic_index_in_dim(
            mixer_weight[layer].reshape(shard, parts, slim), me, 1, keepdims=False
        )
        small = jnp.concatenate(
            [
                item[layer]
                for item in (
                    attend_gain,
                    attend_shift,
                    query_bias,
                    value_bias,
                    mixer_bias,
                    feed_gain,
                    feed_shift,
                    reduce_bias,
                    expand_bias,
                )
            ]
        )
        small = jnp.pad(small, (0, pad_rows * width - small.shape[0])).reshape(pad_rows, width)
        return jnp.concatenate([jnp.concatenate([joint, mixer], axis=1), small], axis=0)

    def own_feed(layer):
        expand = lax.dynamic_index_in_dim(
            expand_weight[layer].reshape(shard, shards, parts, unit), me, 2, keepdims=False
        ).reshape(shard, units)
        reduce = lax.dynamic_slice_in_dim(reduce_weight[layer], me * unit, unit, 0)
        return jnp.concatenate([expand, reduce], axis=0)

    def gather(own):
        return lax.all_gather(own, "fsdp", axis=0, tiled=False)

    def split_joint(whole):
        matrix = whole[:, :shard].reshape(width, width)
        small = whole[:, shard:].reshape(shards, -1).astype(F32)
        vectors = [
            small[:, n * shard : (n + 1) * shard].reshape(width) for n in range(8)
        ]
        expand_b = lax.dynamic_index_in_dim(
            small[:, 8 * shard : 8 * shard + hidden_shard].reshape(shards, parts, unit),
            me,
            1,
            keepdims=False,
        ).reshape(units)
        mixer = gather_ctx(matrix[:, 3 * slim :], me)
        mixer = jnp.transpose(mixer, (1, 0, 2)).reshape(width, width)
        return (matrix[:, : 3 * slim], mixer, vectors, expand_b)

    def split_feed(whole):
        return (
            whole[:, :shard].reshape(width, units),
            whole[:, shard:].reshape(units, width),
        )

    first_joint = gather(own_joint(0))
    first_feed = gather(own_feed(0))
    second_all = gather(jnp.concatenate([own_joint(1), own_feed(1)], axis=0))
    edge = shard + pad_rows
    gathered = (
        (first_joint, first_feed),
        (second_all[:, :edge], second_all[:, edge:]),
    )

    def to_sequence(blocks):
        n = blocks.shape[-1]
        return jnp.transpose(blocks.reshape(parts, seqs, piece, n), (1, 0, 2, 3)).reshape(
            tokens, n
        )

    def from_sequence(array):
        n = array.shape[-1]
        return jnp.transpose(array.reshape(seqs, parts, piece, n), (1, 0, 2, 3)).reshape(
            parts, rows, n
        )

    stream = block_input.astype(F32).reshape(rows, width)
    saved = []
    for layer in range(LAYERS):
        joint_w, mixer_w, vectors, expand_b = split_joint(gathered[layer][0])
        expand_w, reduce_w = split_feed(gathered[layer][1])
        att_gain, att_shift, query_b, value_b, mixer_b, feed_g, feed_s, reduce_b = vectors
        normed, scaled_one, inverse_one = norm_forward(stream, att_gain, att_shift)
        first = to_sequence(gather_ctx(normed.astype(BF), me))
        bias_row = jnp.concatenate(
            [
                lax.dynamic_slice_in_dim(query_b, me * slim, slim),
                jnp.zeros((slim,), F32),
                lax.dynamic_slice_in_dim(value_b, me * slim, slim),
            ]
        )
        joint = (dot(first, joint_w, 1, 0) + bias_row).astype(BF)
        joint = jnp.transpose(joint.reshape(seqs, length, 3 * group, HDIM), (0, 2, 1, 3))
        heads_out = attend_forward(joint)
        attended = lax.all_to_all(heads_out, "ctx", split_axis=2, concat_axis=1, tiled=True)
        attended = jnp.transpose(attended, (0, 2, 1, 3)).reshape(rows, width)
        middle = stream + dot(attended, mixer_w, 1, 0) + mixer_b
        normed_two, scaled_two, inverse_two = norm_forward(middle, feed_g, feed_s)
        second = gather_relative(normed_two.astype(BF)).reshape(tokens, width)
        hidden = dot(second, expand_w, 1, 0) + expand_b
        value, slope = gelu_parts(hidden)
        active = value.astype(BF)
        out = scatter_relative(dot(active, reduce_w, 1, 0).reshape(parts, rows, width))
        stream = middle + out + reduce_b
        saved.append(
            (
                scaled_one,
                inverse_one,
                first,
                joint,
                heads_out,
                attended,
                scaled_two,
                inverse_two,
                second,
                slope,
                active,
                joint_w,
                mixer_w,
                expand_w,
                reduce_w,
                att_gain,
                feed_g,
            )
        )

    upstream = cotangent.astype(F32).reshape(rows, width)
    collected = [None] * LAYERS
    for layer in reversed(range(LAYERS)):
        (
            scaled_one,
            inverse_one,
            first,
            joint,
            heads_out,
            attended,
            scaled_two,
            inverse_two,
            second,
            slope,
            active,
            joint_w,
            mixer_w,
            expand_w,
            reduce_w,
            att_gain,
            feed_g,
        ) = saved[layer]
        reduce_b_grad = jnp.sum(upstream, axis=0)
        up_full = gather_relative(upstream.astype(BF)).reshape(tokens, width)
        hidden_grad = dot(up_full, reduce_w, 1, 1) * slope
        expand_b_grad = jnp.sum(hidden_grad, axis=0)
        hidden_b = hidden_grad.astype(BF)
        into_norm = scatter_relative(dot(hidden_b, expand_w, 1, 1).reshape(parts, rows, width))
        reduce_w_grad = dot(active, up_full, 0, 0).astype(BF)
        expand_w_grad = dot(second, hidden_b, 0, 0).astype(BF)
        norm_grad, feed_g_grad, feed_s_grad = norm_backward(
            into_norm, scaled_two, inverse_two, feed_g
        )
        middle_grad = upstream + norm_grad
        middle_b = middle_grad.astype(BF)
        mixer_b_grad = jnp.sum(middle_grad, axis=0)
        attended_grad = dot(middle_b, mixer_w, 1, 1).astype(BF)
        attended_grad = jnp.transpose(
            attended_grad.reshape(seqs, piece, parts * group, HDIM), (0, 2, 1, 3)
        )
        grad_heads = lax.all_to_all(
            attended_grad, "ctx", split_axis=1, concat_axis=2, tiled=True
        )
        mixer_partial = dot(attended, middle_b, 0, 0).astype(BF)
        mixer_blocks = jnp.transpose(mixer_partial.reshape(width, parts, slim), (1, 0, 2))
        mixer_w_grad = scatter_relative(reorder(mixer_blocks, me)).astype(BF)
        three = attend_backward(joint, heads_out, grad_heads)
        joint_grad = jnp.concatenate(
            [jnp.transpose(item, (0, 2, 1, 3)).reshape(tokens, slim) for item in three], axis=1
        )
        into_partial = from_sequence(dot(joint_grad, joint_w, 1, 1))
        into_first = scatter_relative(reorder(into_partial, me))
        joint_w_grad = dot(first, joint_grad, 0, 0).astype(BF)
        joint_sums = jnp.sum(joint_grad.astype(F32), axis=0)
        first_grad, att_gain_grad, att_shift_grad = norm_backward(
            into_first, scaled_one, inverse_one, att_gain
        )
        upstream = middle_grad + first_grad

        blank = jnp.zeros((width,), F32)
        query_b_grad = lax.dynamic_update_slice(blank, joint_sums[:slim], (me * slim,))
        value_b_grad = lax.dynamic_update_slice(blank, joint_sums[2 * slim :], (me * slim,))
        small = jnp.stack(
            [
                att_gain_grad,
                att_shift_grad,
                query_b_grad,
                value_b_grad,
                mixer_b_grad,
                feed_g_grad,
                feed_s_grad,
                reduce_b_grad,
            ]
        )
        small = jnp.transpose(small.reshape(8, shards, shard), (1, 0, 2)).reshape(shards, 1, -1)
        small = jnp.concatenate([small, expand_b_grad.reshape(shards, 1, unit)], axis=2)
        wide = 3 * width
        small = jnp.pad(
            small.astype(BF), ((0, 0), (0, pad_rows - 1), (0, wide - small.shape[2]))
        )
        big = jnp.concatenate(
            [joint_w_grad, mixer_w_grad, expand_w_grad, reduce_w_grad], axis=1
        ).reshape(shards, shard, wide)
        packed = jnp.concatenate([big, small], axis=1).reshape(shards * edge, wide)
        owned = lax.psum_scatter(packed, "fsdp", scatter_dimension=0, tiled=True)
        whole = gather_ctx(owned, me)
        main = whole[:, :shard].astype(F32)
        thin = whole[:, shard].astype(F32)
        vectors = [
            jnp.sum(thin[:, n * shard : (n + 1) * shard], axis=0) for n in range(8)
        ]
        g_joint = jnp.transpose(
            main[:, :, : 3 * slim].reshape(parts, shard, 3, slim), (1, 2, 0, 3)
        ).reshape(shard, 3 * width)
        g_mixer = jnp.transpose(main[:, :, 3 * slim : width], (1, 0, 2)).reshape(shard, width)
        g_expand = jnp.transpose(
            main[:, :, width : width + units].reshape(parts, shard, shards, unit), (1, 2, 0, 3)
        ).reshape(shard, parts * units)
        g_reduce = main[:, :unit, width + units :].reshape(hidden_shard, width)
        g_expand_b = thin[:, 8 * shard : 8 * shard + unit].reshape(hidden_shard)
        collected[layer] = (
            vectors[0],
            vectors[1],
            g_joint,
            vectors[2],
            vectors[3],
            g_mixer,
            vectors[4],
            vectors[5],
            vectors[6],
            g_expand,
            g_expand_b,
            g_reduce,
            vectors[7],
        )
    grads = tuple(
        jnp.stack([collected[layer][index] for layer in range(LAYERS)]) for index in range(13)
    )
    return (
        stream.reshape(seqs, piece, width),
        upstream.reshape(seqs, piece, width),
    ) + grads


def solution(mesh):
    vector = P(None, "fsdp")
    matrix = P(None, "fsdp", None)
    tokens = P("fsdp", "ctx", None)
    params = (
        vector,
        vector,
        matrix,
        vector,
        vector,
        matrix,
        vector,
        vector,
        vector,
        matrix,
        vector,
        matrix,
        vector,
    )
    return jax.shard_map(
        body,
        mesh=mesh,
        in_specs=(tokens, tokens) + params,
        out_specs=(tokens, tokens) + params,
        check_vma=False,
    )
```

```python
import functools
import math

import jax
import jax.numpy as jnp
from jax import lax
from jax.experimental import pallas as pl
from jax.experimental.pallas import tpu as pltpu
from jax.sharding import PartitionSpec as P

HDIM = 64
LAYERS = 2
EPS = 1e-05
GELU_C = math.sqrt(2.0 / math.pi)
BF = jnp.bfloat16
F32 = jnp.float32
SCALE = 1.0 / math.sqrt(HDIM)


def dot(a, b, da, db):
    return lax.dot_general(a, b, (((da,), (db,)), ((), ())), preferred_element_type=F32)


def norm_forward(stream, gain, shift):
    centred = stream - jnp.mean(stream, axis=-1, keepdims=True)
    inverse = lax.rsqrt(jnp.mean(centred * centred, axis=-1, keepdims=True) + EPS)
    scaled = centred * inverse
    return (scaled * gain + shift, scaled, inverse)


def norm_backward(upstream, scaled, inverse, gain):
    weighted = upstream * gain
    inner = (
        weighted
        - jnp.mean(weighted, axis=-1, keepdims=True)
        - scaled * jnp.mean(weighted * scaled, axis=-1, keepdims=True)
    )
    return (inverse * inner, jnp.sum(upstream * scaled, axis=0), jnp.sum(upstream, axis=0))


def gelu_parts(hidden):
    cube = hidden * hidden * hidden
    tangent = jnp.tanh(GELU_C * (hidden + 0.044715 * cube))
    value = 0.5 * hidden * (1.0 + tangent)
    slope = 0.5 * (1.0 + tangent) + 0.5 * hidden * (1.0 - tangent * tangent) * GELU_C * (
        1.0 + 3.0 * 0.044715 * hidden * hidden
    )
    return (value, slope)


def masked_scores(q, k, start):
    scores = dot(q, k, 1, 1) * SCALE
    rows = start + lax.broadcasted_iota(jnp.int32, scores.shape, 0)
    columns = lax.broadcasted_iota(jnp.int32, scores.shape, 1)
    return jnp.where(columns <= rows, scores, -1e30)


def forward_kernel(block, q_ref, k_ref, v_ref, o_ref):
    for start in range(0, q_ref.shape[0], block):
        end = start + block
        scores = masked_scores(q_ref[start:end, :], k_ref[:end, :], start)
        peak = jnp.max(scores, axis=-1, keepdims=True)
        weights = jnp.exp(scores - peak)
        probs = (weights * (1.0 / jnp.sum(weights, axis=-1, keepdims=True))).astype(BF)
        o_ref[start:end, :] = dot(probs, v_ref[:end, :], 1, 0).astype(BF)


def backward_kernel(block, q_ref, k_ref, v_ref, o_ref, g_ref, dq_ref, dk_ref, dv_ref, ka, va):
    length = q_ref.shape[0]
    for start in reversed(range(0, length, block)):
        end = start + block
        q, k, v, g = q_ref[start:end, :], k_ref[:end, :], v_ref[:end, :], g_ref[start:end, :]
        scores = masked_scores(q, k, start)
        peak = jnp.max(scores, axis=-1, keepdims=True)
        weights = jnp.exp(scores - peak)
        probs = weights * (1.0 / jnp.sum(weights, axis=-1, keepdims=True))
        dv = dot(probs.astype(BF), g, 0, 0)
        delta = jnp.sum(g.astype(F32) * o_ref[start:end, :].astype(F32), axis=-1, keepdims=True)
        ds = (probs * (dot(g, v, 1, 1) - delta)).astype(BF)
        dq_ref[start:end, :] = (dot(ds, k, 1, 0) * SCALE).astype(BF)
        dk = dot(ds, q, 0, 0) * SCALE
        if end == length:
            ka[...] = dk
            va[...] = dv
        else:
            ka[:end, :] += dk
            va[:end, :] += dv
    dk_ref[...] = ka[...].astype(BF)
    dv_ref[...] = va[...].astype(BF)


def head_spec(length, offset):
    return pl.BlockSpec((None, None, length, HDIM), lambda s, h: (s, h + offset, 0, 0))


def attend_forward(joint):
    items, nine, length, _ = joint.shape
    group = nine // 3
    return pl.pallas_call(
        functools.partial(forward_kernel, length // 2),
        grid=(items, group),
        in_specs=[head_spec(length, part * group) for part in range(3)],
        out_specs=head_spec(length, 0),
        out_shape=jax.ShapeDtypeStruct((items, group, length, HDIM), BF),
        cost_estimate=pl.CostEstimate(
            flops=3 * items * group * length * length * HDIM,
            bytes_accessed=8 * items * group * length * HDIM,
            transcendentals=items * group * length * length,
        ),
    )(joint, joint, joint)


def attend_backward(joint, attended, grad):
    items, nine, length, _ = joint.shape
    group = nine // 3
    out = jax.ShapeDtypeStruct((items, group, length, HDIM), BF)
    return pl.pallas_call(
        functools.partial(backward_kernel, length // 2),
        grid=(items, group),
        in_specs=[head_spec(length, part * group) for part in range(3)]
        + [head_spec(length, 0)] * 2,
        out_specs=[head_spec(length, 0)] * 3,
        out_shape=[out] * 3,
        scratch_shapes=[pltpu.VMEM((length, HDIM), F32)] * 2,
        cost_estimate=pl.CostEstimate(
            flops=8 * items * group * length * length * HDIM,
            bytes_accessed=16 * items * group * length * HDIM,
            transcendentals=items * group * length * length,
        ),
    )(joint, joint, joint, attended, grad)


def swap(array, partner):
    return lax.ppermute(array, "ctx", [(i, i ^ partner) for i in range(4)])


def gather_relative(own):
    across = swap(own, 2)
    beside = swap(own, 1)
    return jnp.stack([own, beside, across, swap(across, 1)])


def reorder(blocks, me):
    return jnp.stack(
        [lax.dynamic_index_in_dim(blocks, me ^ r, 0, keepdims=False) for r in range(4)]
    )


def gather_ctx(own, me):
    return reorder(gather_relative(own), me)


def scatter_relative(blocks):
    low = blocks.astype(BF)
    got = swap(jnp.stack([low[1], low[3]]), 1).astype(F32)
    mine = blocks[0].astype(F32) + got[0]
    other = (blocks[2].astype(F32) + got[1]).astype(BF)
    return mine + swap(other, 2).astype(F32)


def body(
    block_input,
    cotangent,
    attend_gain,
    attend_shift,
    joint_weight,
    query_bias,
    value_bias,
    mixer_weight,
    mixer_bias,
    feed_gain,
    feed_shift,
    expand_weight,
    expand_bias,
    reduce_weight,
    reduce_bias,
):
    me = lax.axis_index("ctx")
    parts = 4
    shards = lax.axis_size("fsdp")
    seqs, piece, width = block_input.shape
    rows = seqs * piece
    tokens = rows * parts
    length = piece * parts
    slim = width // parts
    group = slim // HDIM
    shard = width // shards
    hidden_shard = reduce_weight.shape[1]
    unit = hidden_shard // parts
    units = unit * shards
    pad_rows = 8

    def own_joint(layer):
        joint = lax.dynamic_index_in_dim(
            joint_weight[layer].reshape(shard, 3, parts, slim), me, 2, keepdims=False
        ).reshape(shard, 3 * slim)
        mixer = lax.dynamic_index_in_dim(
            mixer_weight[layer].reshape(shard, parts, slim), me, 1, keepdims=False
        )
        small = jnp.concatenate(
            [
                item[layer]
                for item in (
                    attend_gain,
                    attend_shift,
                    query_bias,
                    value_bias,
                    mixer_bias,
                    feed_gain,
                    feed_shift,
                    reduce_bias,
                    expand_bias,
                )
            ]
        )
        small = jnp.pad(small, (0, pad_rows * width - small.shape[0])).reshape(pad_rows, width)
        return jnp.concatenate([jnp.concatenate([joint, mixer], axis=1), small], axis=0)

    def own_feed(layer):
        expand = lax.dynamic_index_in_dim(
            expand_weight[layer].reshape(shard, shards, parts, unit), me, 2, keepdims=False
        ).reshape(shard, units)
        reduce = lax.dynamic_slice_in_dim(reduce_weight[layer], me * unit, unit, 0)
        return jnp.concatenate([expand, reduce], axis=0)

    def gather(own):
        return lax.all_gather(own, "fsdp", axis=0, tiled=False)

    def split_joint(whole):
        matrix = whole[:, :shard].reshape(width, width)
        small = whole[:, shard:].reshape(shards, -1).astype(F32)
        vectors = [
            small[:, n * shard : (n + 1) * shard].reshape(width) for n in range(8)
        ]
        expand_b = lax.dynamic_index_in_dim(
            small[:, 8 * shard : 8 * shard + hidden_shard].reshape(shards, parts, unit),
            me,
            1,
            keepdims=False,
        ).reshape(units)
        mixer = gather_ctx(matrix[:, 3 * slim :], me)
        mixer = jnp.transpose(mixer, (1, 0, 2)).reshape(width, width)
        return (matrix[:, : 3 * slim], mixer, vectors, expand_b)

    def split_feed(whole):
        return (
            whole[:, :shard].reshape(width, units),
            whole[:, shard:].reshape(units, width),
        )

    first_joint = gather(own_joint(0))
    first_feed = gather(own_feed(0))
    edge = shard + pad_rows
    gathered = [(first_joint, first_feed), None]
    second_own = jnp.concatenate([own_joint(1), own_feed(1)], axis=0)

    def to_sequence(blocks):
        n = blocks.shape[-1]
        return jnp.transpose(blocks.reshape(parts, seqs, piece, n), (1, 0, 2, 3)).reshape(
            tokens, n
        )

    def from_sequence(array):
        n = array.shape[-1]
        return jnp.transpose(array.reshape(seqs, parts, piece, n), (1, 0, 2, 3)).reshape(
            parts, rows, n
        )

    stream = block_input.astype(F32).reshape(rows, width)
    saved = []
    for layer in range(LAYERS):
        joint_w, mixer_w, vectors, expand_b = split_joint(gathered[layer][0])
        expand_w, reduce_w = split_feed(gathered[layer][1])
        att_gain, att_shift, query_b, value_b, mixer_b, feed_g, feed_s, reduce_b = vectors
        normed, scaled_one, inverse_one = norm_forward(stream, att_gain, att_shift)
        first = to_sequence(gather_ctx(normed.astype(BF), me))
        bias_row = jnp.concatenate(
            [
                lax.dynamic_slice_in_dim(query_b, me * slim, slim),
                jnp.zeros((slim,), F32),
                lax.dynamic_slice_in_dim(value_b, me * slim, slim),
            ]
        )
        joint = (dot(first, joint_w, 1, 0) + bias_row).astype(BF)
        if layer == 0:
            joint, second_own = lax.optimization_barrier((joint, second_own))
            second_all = gather(second_own)
            gathered[1] = (second_all[:, :edge], second_all[:, edge:])
        joint = jnp.transpose(joint.reshape(seqs, length, 3 * group, HDIM), (0, 2, 1, 3))
        heads_out = attend_forward(joint)
        attended = lax.all_to_all(heads_out, "ctx", split_axis=2, concat_axis=1, tiled=True)
        attended = jnp.transpose(attended, (0, 2, 1, 3)).reshape(rows, width)
        middle = stream + dot(attended, mixer_w, 1, 0) + mixer_b
        normed_two, scaled_two, inverse_two = norm_forward(middle, feed_g, feed_s)
        second = gather_relative(normed_two.astype(BF)).reshape(tokens, width)
        hidden = dot(second, expand_w, 1, 0) + expand_b
        value, slope = gelu_parts(hidden)
        active = value.astype(BF)
        out = scatter_relative(dot(active, reduce_w, 1, 0).reshape(parts, rows, width))
        stream = middle + out + reduce_b
        saved.append(
            (
                scaled_one,
                inverse_one,
                first,
                joint,
                heads_out,
                attended,
                scaled_two,
                inverse_two,
                second,
                slope,
                active,
                joint_w,
                mixer_w,
                expand_w,
                reduce_w,
                att_gain,
                feed_g,
            )
        )

    upstream = cotangent.astype(F32).reshape(rows, width)
    collected = [None] * LAYERS
    for layer in reversed(range(LAYERS)):
        (
            scaled_one,
            inverse_one,
            first,
            joint,
            heads_out,
            attended,
            scaled_two,
            inverse_two,
            second,
            slope,
            active,
            joint_w,
            mixer_w,
            expand_w,
            reduce_w,
            att_gain,
            feed_g,
        ) = saved[layer]
        reduce_b_grad = jnp.sum(upstream, axis=0)
        up_full = gather_relative(upstream.astype(BF)).reshape(tokens, width)
        hidden_grad = dot(up_full, reduce_w, 1, 1) * slope
        expand_b_grad = jnp.sum(hidden_grad, axis=0)
        hidden_b = hidden_grad.astype(BF)
        into_norm = scatter_relative(dot(hidden_b, expand_w, 1, 1).reshape(parts, rows, width))
        reduce_w_grad = dot(active, up_full, 0, 0).astype(BF)
        expand_w_grad = dot(second, hidden_b, 0, 0).astype(BF)
        norm_grad, feed_g_grad, feed_s_grad = norm_backward(
            into_norm, scaled_two, inverse_two, feed_g
        )
        middle_grad = upstream + norm_grad
        middle_b = middle_grad.astype(BF)
        mixer_b_grad = jnp.sum(middle_grad, axis=0)
        attended_grad = dot(middle_b, mixer_w, 1, 1).astype(BF)
        attended_grad = jnp.transpose(
            attended_grad.reshape(seqs, piece, parts * group, HDIM), (0, 2, 1, 3)
        )
        grad_heads = lax.all_to_all(
            attended_grad, "ctx", split_axis=1, concat_axis=2, tiled=True
        )
        mixer_partial = dot(attended, middle_b, 0, 0).astype(BF)
        mixer_blocks = jnp.transpose(mixer_partial.reshape(width, parts, slim), (1, 0, 2))
        mixer_w_grad = scatter_relative(reorder(mixer_blocks, me)).astype(BF)
        three = attend_backward(joint, heads_out, grad_heads)
        joint_grad = jnp.concatenate(
            [jnp.transpose(item, (0, 2, 1, 3)).reshape(tokens, slim) for item in three], axis=1
        )
        into_partial = from_sequence(dot(joint_grad, joint_w, 1, 1))
        into_first = scatter_relative(reorder(into_partial, me))
        joint_w_grad = dot(first, joint_grad, 0, 0).astype(BF)
        joint_sums = jnp.sum(joint_grad.astype(F32), axis=0)
        first_grad, att_gain_grad, att_shift_grad = norm_backward(
            into_first, scaled_one, inverse_one, att_gain
        )
        upstream = middle_grad + first_grad

        blank = jnp.zeros((width,), F32)
        query_b_grad = lax.dynamic_update_slice(blank, joint_sums[:slim], (me * slim,))
        value_b_grad = lax.dynamic_update_slice(blank, joint_sums[2 * slim :], (me * slim,))
        small = jnp.stack(
            [
                att_gain_grad,
                att_shift_grad,
                query_b_grad,
                value_b_grad,
                mixer_b_grad,
                feed_g_grad,
                feed_s_grad,
                reduce_b_grad,
            ]
        )
        small = jnp.transpose(small.reshape(8, shards, shard), (1, 0, 2)).reshape(shards, 1, -1)
        small = jnp.concatenate([small, expand_b_grad.reshape(shards, 1, unit)], axis=2)
        wide = 3 * width
        small = jnp.pad(
            small.astype(BF), ((0, 0), (0, pad_rows - 1), (0, wide - small.shape[2]))
        )
        big = jnp.concatenate(
            [joint_w_grad, mixer_w_grad, expand_w_grad, reduce_w_grad], axis=1
        ).reshape(shards, shard, wide)
        packed = jnp.concatenate([big, small], axis=1).reshape(shards * edge, wide)
        owned = lax.psum_scatter(packed, "fsdp", scatter_dimension=0, tiled=True)
        whole = gather_ctx(owned, me)
        main = whole[:, :shard].astype(F32)
        thin = whole[:, shard].astype(F32)
        vectors = [
            jnp.sum(thin[:, n * shard : (n + 1) * shard], axis=0) for n in range(8)
        ]
        g_joint = jnp.transpose(
            main[:, :, : 3 * slim].reshape(parts, shard, 3, slim), (1, 2, 0, 3)
        ).reshape(shard, 3 * width)
        g_mixer = jnp.transpose(main[:, :, 3 * slim : width], (1, 0, 2)).reshape(shard, width)
        g_expand = jnp.transpose(
            main[:, :, width : width + units].reshape(parts, shard, shards, unit), (1, 2, 0, 3)
        ).reshape(shard, parts * units)
        g_reduce = main[:, :unit, width + units :].reshape(hidden_shard, width)
        g_expand_b = thin[:, 8 * shard : 8 * shard + unit].reshape(hidden_shard)
        collected[layer] = (
            vectors[0],
            vectors[1],
            g_joint,
            vectors[2],
            vectors[3],
            g_mixer,
            vectors[4],
            vectors[5],
            vectors[6],
            g_expand,
            g_expand_b,
            g_reduce,
            vectors[7],
        )
    grads = tuple(
        jnp.stack([collected[layer][index] for layer in range(LAYERS)]) for index in range(13)
    )
    return (
        stream.reshape(seqs, piece, width),
        upstream.reshape(seqs, piece, width),
    ) + grads


def solution(mesh):
    vector = P(None, "fsdp")
    matrix = P(None, "fsdp", None)
    tokens = P("fsdp", "ctx", None)
    params = (
        vector,
        vector,
        matrix,
        vector,
        vector,
        matrix,
        vector,
        vector,
        vector,
        matrix,
        vector,
        matrix,
        vector,
    )
    return jax.shard_map(
        body,
        mesh=mesh,
        in_specs=(tokens, tokens) + params,
        out_specs=(tokens, tokens) + params,
        check_vma=False,
    )
```
